32 devices in a mesh: clip: 4 (over z), sp: 4 (over x, core), tp: 2 (over y).
Axes of the slice: x: 2, y: 2, z: 4, core: 2. Of those that a mesh axis runs over, the one named last changes fastest.
Arguments:
- latents: bfloat16 [4, 4, 1024, 512], P('clip', 'sp', None, 'tp'), may hold values from -6 to 6
- saved_input: bfloat16 [4, 4, 1024, 512], P('clip', None, 'sp', 'tp'), may hold values from -6 to 6
- out_grad: bfloat16 [4, 4, 1024, 512], P('clip', None, 'sp', 'tp'), may hold values from -6 to 6
- temporal_weight: bfloat16 [3, 512, 512], P(None, 'tp'), may hold values from -0.15625 to 0.15625
- spatial_weight: bfloat16 [9, 512, 512], P(None, 'tp'), may hold values from -0.09375 to 0.09375
Outputs:
- input_grad: bfloat16 [4, 4, 1024, 512], P('clip', 'sp', None, 'tp')
- temporal_grad: float32 [3, 512, 512], P(None, 'tp', 'sp')
- spatial_grad: float32 [9, 512, 512], P(None, 'tp', 'sp')
The draws below stay inside these ranges and needn't reach their ends.
All inputs are finite; a program needn't handle non-finite values.
Results may differ from the reference program's by a relative error of at most 0.005.
Values may be sent and summed in bfloat16 or wider, within the bound.
A program may use at most 64 MiB of HBM per device.

```python
import jax
import jax.numpy as jnp
from jax import lax

C = 512
HS = 32
WS = 32
FRAMES = 4
CLIPS = 4
HW = 1024


def with_spikes(values, rng, source, target, blocks, factor):
    owner, partner = [(jnp.arange(values.shape[axis_at]) // (values.shape[axis_at] // blocks)).reshape([-1 if axis == axis_at else 1 for axis in range(values.ndim)]) for axis_at in (source, target)]
    chosen = jax.random.permutation(rng, blocks)[partner]
    strong = (owner == chosen) | (owner == (partner + blocks // 2) % blocks)
    return jnp.where(strong, factor * values, values)


def steps_of(stream_key, dims, split, low, top_value):
    factor_of, own = 1.0, jax.random.fold_in(stream_key, 6)
    for axis_at, parts in split:
        heights = jnp.exp(jax.random.uniform(jax.random.fold_in(own, axis_at), (parts,), jnp.float32, low / len(split), top_value / len(split)))
        factor_of = factor_of * jnp.repeat(heights, dims[axis_at] // parts).reshape([-1 if axis == axis_at else 1 for axis in range(len(dims))])
    return factor_of


def noise(key, extent, scale, limit, cuts=(), kind=jnp.bfloat16):
    factor_of = steps_of(key, extent, cuts, -0.22, 0.18) if cuts else 1.0
    values = jax.random.normal(key, extent, jnp.float32) * scale * factor_of
    return jnp.minimum(jnp.maximum(values, -limit), limit).astype(kind)


def heavy_noise(stream_key, shape, scale, limit, shards, heavy, dtype=jnp.bfloat16):
    array = scale * jax.random.normal(stream_key, shape, jnp.float32)
    if shards:
        array = array * steps_of(stream_key, shape, shards, -0.22, 0.18)
    return jnp.clip(with_spikes(array, jax.random.fold_in(stream_key, 3), *heavy), -limit, limit).astype(dtype)


def setup_inputs(seed: int = 0) -> dict:
    splits = jax.random.split(jax.random.key(seed), 6)
    return {
        "latents": noise(splits[0], (CLIPS, FRAMES, HW, C), 1.0, 6.0, ((0, 4), (1, 4), (3, 2))),
        "saved_input": noise(splits[1], (CLIPS, FRAMES, HW, C), 1.0, 6.0, ((0, 4), (2, 4), (3, 2))),
        "out_grad": heavy_noise(splits[2], (CLIPS, FRAMES, HW, C), 1.0, 6.0, ((0, 4), (2, 4), (3, 2)), (2, 3, 4, 2.0)),
        "temporal_weight": noise(splits[3], (3, C, C), (3 * C) ** -0.5, 0.15625, ((1, 2),)),
        "spatial_weight": noise(splits[4], (9, C, C), (9 * C) ** -0.5, 0.09375, ((1, 2),)),
    }


def reference(latents, saved_input, out_grad, temporal_weight, spatial_weight):
    clips, frames, cells, width = latents.shape
    temporal_full = temporal_weight.astype(jnp.float32)
    spatial_full = spatial_weight.astype(jnp.float32)

    def one_clip(index):
        grad_out = out_grad[index].astype(jnp.float32)
        saved = saved_input[index].astype(jnp.float32)
        image = latents[index].astype(jnp.float32)
        grad_pad = jnp.pad(grad_out, ((1, 1), (0, 0), (0, 0)))
        saved_pad = jnp.pad(saved, ((1, 1), (0, 0), (0, 0)))
        hidden_acc = jnp.zeros((frames, cells, width), jnp.float32)
        temporal_parts = []
        for tap_index in range(3):
            shifted = grad_pad[2 - tap_index:2 - tap_index + frames]
            hidden_acc = hidden_acc + jnp.einsum('fpo,io->fpi', shifted, temporal_full[tap_index])
            temporal_parts.append(jnp.einsum('fpi,fpo->io', saved_pad[tap_index:tap_index + frames], grad_out))
        hidden_grad = lax.optimization_barrier(hidden_acc.astype(jnp.bfloat16)).astype(jnp.float32)
        grid = jnp.pad(hidden_grad.reshape(frames, HS, WS, width), ((0, 0), (1, 1), (1, 1), (0, 0)))
        image_pad = jnp.pad(image.reshape(frames, HS, WS, width), ((0, 0), (1, 1), (1, 1), (0, 0)))
        plain = hidden_grad.reshape(frames, HS, WS, width)
        input_acc = jnp.zeros((frames, HS, WS, width), jnp.float32)
        spatial_parts = []
        for row_shift in (-1, 0, 1):
            for col_shift in (-1, 0, 1):
                tap_index = 3 * (row_shift + 1) + (col_shift + 1)
                moved = grid[:, 1 - row_shift:1 - row_shift + HS, 1 - col_shift:1 - col_shift + WS]
                input_acc = input_acc + jnp.einsum('gabo,co->gabc', moved, spatial_full[tap_index])
                window = image_pad[:, 1 + row_shift:1 + row_shift + HS, 1 + col_shift:1 + col_shift + WS]
                spatial_parts.append(jnp.einsum('gabc,gabo->co', window, plain))
        result = input_acc.reshape(frames, cells, width).astype(jnp.bfloat16)
        return (result, jnp.stack(temporal_parts), jnp.stack(spatial_parts))
    input_grad, temporal_terms, spatial_terms = lax.map(one_clip, jnp.arange(clips))
    scale_factor = 1.0 / jnp.sqrt(jnp.float32(clips * frames * cells))
    temporal_grad = lax.optimization_barrier(jnp.sum(temporal_terms, axis=0)) * scale_factor
    spatial_grad = lax.optimization_barrier(jnp.sum(spatial_terms, axis=0)) * scale_factor
    return (input_grad, temporal_grad, spatial_grad)
```

```python
import functools
import math

import jax
import jax.numpy as jnp
from jax import lax
from jax.experimental import pallas as pl
from jax.experimental.pallas import tpu as pltpu
from jax.sharding import PartitionSpec as P

HS = 32
WS = 32
MESH = pl.DeviceIdType.MESH
F32 = jnp.float32
BF16 = jnp.bfloat16


def pad_frames(values):
    return jnp.pad(values, ((0, 0), (1, 1), (0, 0), (0, 0)))


def nt(a, b):
    return lax.dot_general(a, b, (((1,), (1,)), ((), ())), preferred_element_type=F32)


def nn(a, b):
    return lax.dot_general(a, b, (((1,), (0,)), ((), ())), preferred_element_type=F32)


def chunks_of(taps, size):
    return [(start, min(size, taps - start)) for start in range(0, taps, size)]


def kernel(
    dims, lat, sav, og, tw, sw, ig, tg, sg,
    latv, savv, twv, swv, opad, hsend, hrecv, hwide, hs, savt, latt, acc,
    gsend, g1, g2s, g2r, gz, g3r, gq, gf,
    lsem, osend, orecv, osem, hsendsem, hrecvsem, hlocsem,
    s1s, s1r, s2s, s2r, s3s, s3r, s4s, s4r,
):
    S, T, Z, F, Pl, Cl, Cs, scale, chunks, KT = dims
    U = S // 2
    Q = Cl // Z
    HW = S * Pl
    C = T * Cl
    me_s, me_t, me_z = lax.axis_index("sp"), lax.axis_index("tp"), lax.axis_index("clip")
    me_u, me_c = me_s // 2, lax.rem(me_s, 2)

    loads = [
        pltpu.make_async_copy(src, dst, lsem.at[n])
        for n, (src, dst) in enumerate(((sav, savv), (tw, twv), (lat, latv), (sw, swv)))
    ]
    for copy in loads:
        copy.start()
    my_cols = pl.ds(pl.multiple_of(me_t * Cl, Cl), Cl)
    mine = [
        pltpu.make_async_copy(og.at[pl.ds(f * Pl, Pl)], opad.at[pl.ds((f + 1) * Pl, Pl), my_cols], osem.at[f])
        for f in range(F)
    ]
    for copy in mine:
        copy.start()

    barrier = pltpu.get_barrier_semaphore()
    count = 0
    for ds_ in range(S):
        for dt in range(T):
            if ds_ == 0 and dt == 0:
                continue
            count += 1
            pl.semaphore_signal(
                barrier, inc=1, device_id=(me_z, lax.rem(me_s + ds_, S), lax.rem(me_t + dt, T)),
                device_id_type=MESH,
            )
    for dz in range(1, Z):
        count += 1
        pl.semaphore_signal(
            barrier, inc=1, device_id=(lax.rem(me_z + dz, Z), me_s, me_t), device_id_type=MESH
        )
    pl.semaphore_wait(barrier, count)

    ocopies = []
    for d in range(F):
        f = lax.rem(me_s + d, F)
        for dt in range(1, T):
            copy = pltpu.make_async_remote_copy(
                src_ref=og.at[pl.ds(pl.multiple_of(f * Pl, Pl), Pl)],
                dst_ref=opad.at[pl.ds(pl.multiple_of((f + 1) * Pl, Pl), Pl), my_cols],
                send_sem=osend.at[d, dt - 1], recv_sem=orecv.at[d, dt - 1],
                device_id=(me_z, me_s, lax.rem(me_t + dt, T)), device_id_type=MESH,
            )
            copy.start()
            ocopies.append(copy)

    opad[pl.ds(0, Pl), :] = jnp.zeros((Pl, C), BF16)
    opad[pl.ds((F + 1) * Pl, Pl), :] = jnp.zeros((Pl, C), BF16)
    hwide[pl.ds(0, 8), :] = jnp.zeros((8, C), F32)
    hwide[pl.ds(8 + HW, 8), :] = jnp.zeros((8, C), F32)
    for b in range(3):
        hs[b, pl.ds(0, WS), :] = jnp.zeros((WS, C), BF16)
        hs[b, pl.ds(WS + HW, WS), :] = jnp.zeros((WS, C), BF16)
    loads[0].wait()
    savt[...] = savv[...].T
    loads[2].wait()
    latt[...] = latv[...].T
    loads[1].wait()
    loads[3].wait()
    for copy in mine:
        copy.wait()
    for copy in ocopies:
        copy.wait()

    hcopies = []
    for d in list(range(1, S)) + [0]:
        f = lax.rem(me_s + d, S)
        rows = pl.ds(pl.multiple_of(f * Pl, Pl), Pl)
        total = None
        for k in range(KT):
            moved = opad[pl.ds(pl.multiple_of((f + KT - 1 - k) * Pl, Pl), Pl), :]
            term = nt(moved, twv[k])
            total = term if total is None else total + term
        hsend[rows, :] = total.astype(BF16)
        dst = hrecv.at[pl.ds(pl.multiple_of(me_s * Pl, Pl), Pl), my_cols]
        for dt in range(T):
            if d == 0 and dt == 0:
                own = pltpu.make_async_copy(hsend.at[rows], dst, hlocsem)
                own.start()
                continue
            copy = pltpu.make_async_remote_copy(
                src_ref=hsend.at[rows], dst_ref=dst,
                send_sem=hsendsem.at[d, dt], recv_sem=hrecvsem.at[d, dt],
                device_id=(me_z, f, lax.rem(me_t + dt, T)), device_id_type=MESH,
            )
            copy.start()
            hcopies.append(copy)

    sent = {}

    def store_partial(tap, part):
        for s in range(S):
            gsend[s % 2, s // 2, tap] = part[:, s * Cs : (s + 1) * Cs].astype(BF16)

    def start1(n):
        at, size = chunks[n]
        copy = pltpu.make_async_remote_copy(
            src_ref=gsend.at[1 - me_c, :, pl.ds(at, size)], dst_ref=g1.at[:, pl.ds(at, size)],
            send_sem=s1s.at[n], recv_sem=s1r.at[n],
            device_id=(me_z, me_u * 2 + 1 - me_c, me_t), device_id_type=MESH,
        )
        copy.start()
        sent[1, n] = [copy]

    def step1(n):
        at, size = chunks[n]
        taps = pl.ds(at, size)
        for copy in sent[1, n]:
            copy.wait()
        g2s[:, taps] = (gsend[me_c, :, taps].astype(F32) + g1[:, taps].astype(F32)).astype(BF16)
        copies = []
        for d in range(1, U):
            other = lax.rem(me_u + d, U)
            copy = pltpu.make_async_remote_copy(
                src_ref=g2s.at[other, taps], dst_ref=g2r.at[d - 1, taps],
                send_sem=s2s.at[n, d - 1], recv_sem=s2r.at[n, d - 1],
                device_id=(me_z, other * 2 + me_c, me_t), device_id_type=MESH,
            )
            copy.start()
            copies.append(copy)
        sent[2, n] = copies

    def step2(n):
        at, size = chunks[n]
        taps = pl.ds(at, size)
        for copy in sent[2, n]:
            copy.wait()
        total = g2s[me_u, taps].astype(F32)
        for d in range(1, U):
            total = total + g2r[d - 1, taps].astype(F32)
        gz[taps] = total.astype(BF16)
        copies = []
        for d in range(1, Z):
            other = lax.rem(me_z + d, Z)
            copy = pltpu.make_async_remote_copy(
                src_ref=gz.at[taps, pl.ds(pl.multiple_of(other * Q, Q), Q)],
                dst_ref=g3r.at[d - 1, taps],
                send_sem=s3s.at[n, d - 1], recv_sem=s3r.at[n, d - 1],
                device_id=(other, me_s, me_t), device_id_type=MESH,
            )
            copy.start()
            copies.append(copy)
        sent[3, n] = copies

    def step3(n):
        at, size = chunks[n]
        taps = pl.ds(at, size)
        rows = pl.ds(pl.multiple_of(me_z * Q, Q), Q)
        for copy in sent[3, n]:
            copy.wait()
        total = gz[taps, rows].astype(F32)
        for d in range(1, Z):
            total = total + g3r[d - 1, taps].astype(F32)
        total = total.astype(BF16)
        gq[taps] = total
        gf[taps, rows] = total
        copies = []
        for d in range(1, Z):
            copy = pltpu.make_async_remote_copy(
                src_ref=gq.at[taps], dst_ref=gf.at[taps, rows],
                send_sem=s4s.at[n, d - 1], recv_sem=s4r.at[n, d - 1],
                device_id=(lax.rem(me_z + d, Z), me_s, me_t), device_id_type=MESH,
            )
            copy.start()
            copies.append(copy)
        sent[4, n] = copies

    def step4(n):
        at, size = chunks[n]
        for copy in sent[4, n]:
            copy.wait()
        value = gf[pl.ds(at, size)].astype(F32) * scale
        if at < KT:
            tg[pl.ds(at, size)] = value
        else:
            sg[pl.ds(at - KT, size)] = value

    first = len([0 for at, _ in chunks if at < KT])
    for n in range(first):
        at, size = chunks[n]

        @pl.loop(at, at + size)
        def _(k):
            moved = opad[pl.ds(pl.multiple_of((KT - 1 - k) * Pl, Pl), F * Pl), :]
            store_partial(k, nn(savt[...], moved))

        start1(n)
    for n in range(first):
        step1(n)

    own.wait()
    for copy in hcopies:
        copy.wait()

    tile = 4 * WS
    for r in range(0, HW, tile):
        hwide[pl.ds(8 + r, tile), :] = hrecv[pl.ds(r, tile), :].astype(F32)
        hs[1, pl.ds(WS + r, tile), :] = hrecv[pl.ds(r, tile), :]
    column = lax.rem(lax.broadcasted_iota(jnp.int32, (tile, C), 0), WS)
    for b in (-1, 1):
        keep = column != (0 if b == 1 else WS - 1)
        for r in range(0, HW, tile):
            value = hwide[pl.ds(8 + r - b, tile), :]
            hs[b + 1, pl.ds(WS + r, tile), :] = jnp.where(keep, value, 0.0).astype(BF16)

    def moved_at(tap):
        row, col = tap // 3, lax.rem(tap, 3)
        return hs[col, pl.ds(pl.multiple_of((2 - row) * WS, WS), HW), :]

    def gradient(n):
        at, size = chunks[n]

        @pl.loop(at - KT, at - KT + size)
        def _(tap):
            store_partial(tap + KT, nn(latt[...], moved_at(tap)))

        start1(n)

    def image(lo, hi):
        @pl.loop(lo, hi)
        def _(tap):
            term = nt(moved_at(tap), swv[tap])
            if lo == 0:
                @pl.when(tap == 0)
                def _():
                    acc[...] = term

                @pl.when(tap > 0)
                def _():
                    acc[...] += term
            else:
                acc[...] += term

    total = len(chunks)
    work = [("g", n) for n in range(first, total)] + [("i", n) for n in range(3)]
    done = {n: 1 for n in range(first)}
    for kind, n in work:
        if kind == "g":
            gradient(n)
        else:
            image(3 * n, 3 * n + 3)
        for m in range(total):
            if m in done and done[m] < 4:
                done[m] += 1
                (None, step1, step2, step3, step4)[done[m]](m)
        if kind == "g":
            done[n] = 0
    ig[...] = acc[...].astype(BF16)
    while any(done[m] < 4 for m in done):
        for m in range(total):
            if done[m] < 4:
                done[m] += 1
                (None, step1, step2, step3, step4)[done[m]](m)


def fused(sizes, chunk, latents, saved_input, out_grad, temporal_weight, spatial_weight):
    S, T, Z = sizes
    F, Pl, Cl = out_grad.shape[1:]
    KT, _, C = temporal_weight.shape
    taps = KT + spatial_weight.shape[0]
    HW = latents.shape[2]
    Cs = C // S
    U, Q = S // 2, Cl // Z
    scale = 1.0 / math.sqrt(Z * F * HS * WS)
    chunks = chunks_of(KT, chunk) + [(KT + at, n) for at, n in chunks_of(taps - KT, chunk)]
    N = len(chunks)
    dims = (S, T, Z, F, Pl, Cl, Cs, scale, chunks, KT)
    V = pltpu.VMEM
    D = pltpu.SemaphoreType.DMA
    hbm = pl.BlockSpec(memory_space=pl.ANY)
    vmem = pl.BlockSpec(memory_space=pltpu.VMEM)
    ig, tg, sg = pl.pallas_call(
        functools.partial(kernel, dims),
        out_shape=(
            jax.ShapeDtypeStruct((HW, Cl), BF16),
            jax.ShapeDtypeStruct((KT, Cl, Cs), F32),
            jax.ShapeDtypeStruct((taps - KT, Cl, Cs), F32),
        ),
        in_specs=[hbm] * 5,
        out_specs=(vmem,) * 3,
        scratch_shapes=[
            V((HW, Cl), BF16), V((F * Pl, Cl), BF16), V((KT, Cl, C), BF16), V((taps - KT, Cl, C), BF16),
            V(((F + 2) * Pl, C), BF16), V((F * Pl, Cl), BF16), V((HW, C), BF16),
            V((HW + 16, C), F32), V((3, HW + 2 * WS, C), BF16),
            V((Cl, F * Pl), BF16), V((Cl, HW), BF16), V((HW, Cl), F32),
            V((2, U, taps, Cl, Cs), BF16), V((U, taps, Cl, Cs), BF16), V((U, taps, Cl, Cs), BF16),
            V((U - 1, taps, Cl, Cs), BF16), V((taps, Cl, Cs), BF16), V((Z - 1, taps, Q, Cs), BF16),
            V((taps, Q, Cs), BF16), V((taps, Cl, Cs), BF16),
            D((4,)), D((F, T - 1)), D((F, T - 1)), D((F,)), D((S, T)), D((S, T)), D(()),
            D((N,)), D((N,)), D((N, U - 1)), D((N, U - 1)),
            D((N, Z - 1)), D((N, Z - 1)), D((N, Z - 1)), D((N, Z - 1)),
        ],
        compiler_params=pltpu.CompilerParams(
            collective_id=0, has_side_effects=True, vmem_limit_bytes=60 * 2**20
        ),
    )(
        latents.reshape(HW, Cl), saved_input.reshape(F * Pl, Cl), out_grad.reshape(F * Pl, Cl),
        temporal_weight, spatial_weight,
    )
    return ig.reshape(latents.shape), tg, sg


def plain(latents, saved_input, out_grad, temporal_weight, spatial_weight):
    clips_all = latents.shape[0] * lax.axis_size("clip")
    frames_all = latents.shape[1] * lax.axis_size("sp")
    scale_factor = 1.0 / math.sqrt(clips_all * frames_all * HS * WS)
    frames_count = out_grad.shape[1]
    local_in = temporal_weight.shape[1]
    saved_padded = pad_frames(saved_input)
    block_in = lax.all_gather(out_grad, "tp", axis=3, tiled=True)
    padded = pad_frames(block_in)
    hidden_acc = jnp.zeros(out_grad.shape[:3] + (local_in,), F32)
    parts = []
    for tap_index in range(3):
        shifted = padded[:, 2 - tap_index : 2 - tap_index + frames_count]
        hidden_acc = hidden_acc + jnp.einsum(
            "bfpo,io->bfpi", shifted, temporal_weight[tap_index], preferred_element_type=F32
        )
        window = saved_padded[:, tap_index : tap_index + frames_count]
        parts.append(jnp.einsum("bfpi,bfpo->io", window, block_in, preferred_element_type=F32))
    temporal_local = jnp.stack(parts)
    hidden_grad = hidden_acc.astype(BF16)
    regrouped = lax.all_to_all(hidden_grad, "sp", split_axis=1, concat_axis=2, tiled=True)
    batch = latents.shape[0] * latents.shape[1]
    image_pad = jnp.pad(latents.reshape(batch, HS, WS, local_in), ((0, 0), (1, 1), (1, 1), (0, 0)))
    block_in = lax.all_gather(regrouped, "tp", axis=3, tiled=True)
    whole = block_in.reshape(batch, HS, WS, block_in.shape[3])
    grid = jnp.pad(whole, ((0, 0), (1, 1), (1, 1), (0, 0)))
    input_acc = jnp.zeros((batch, HS, WS, local_in), F32)
    parts = []
    for row in (-1, 0, 1):
        for col in (-1, 0, 1):
            tap_index = 3 * (row + 1) + (col + 1)
            moved = grid[:, 1 - row : 1 - row + HS, 1 - col : 1 - col + WS]
            input_acc = input_acc + jnp.einsum(
                "gabo,co->gabc", moved, spatial_weight[tap_index], preferred_element_type=F32
            )
            window = image_pad[:, 1 + row : 1 + row + HS, 1 + col : 1 + col + WS]
            parts.append(jnp.einsum("gabc,gabo->co", window, whole, preferred_element_type=F32))
    spatial_local = jnp.stack(parts)
    input_grad = input_acc.reshape(latents.shape).astype(BF16)
    temporal_grad, spatial_grad = lax.psum(
        tuple(
            lax.psum_scatter(value * scale_factor, "sp", scatter_dimension=2, tiled=True)
            for value in (temporal_local, spatial_local)
        ),
        "clip",
    )
    return input_grad, temporal_grad, spatial_grad


CHUNK = 3


def solution(mesh):
    sizes = (mesh.shape["sp"], mesh.shape["tp"], mesh.shape["clip"])

    def local(latents, saved_input, out_grad, temporal_weight, spatial_weight):
        S, T, Z = sizes
        cols = temporal_weight.shape[2] // S
        fits = (
            latents.shape[:2] == (1, 1) and S % 2 == 0 and S > 2 and T > 1 and Z > 1
            and cols % 128 == 0 and out_grad.shape[3] % (16 * Z) == 0 and out_grad.shape[3] % 128 == 0
        )
        args = (latents, saved_input, out_grad, temporal_weight, spatial_weight)
        return fused(sizes, CHUNK, *args) if fits else plain(*args)

    return jax.shard_map(
        local,
        mesh=mesh,
        in_specs=(
            P("clip", "sp", None, "tp"),
            P("clip", None, "sp", "tp"),
            P("clip", None, "sp", "tp"),
            P(None, "tp", None),
            P(None, "tp", None),
        ),
        out_specs=(P("clip", "sp", None, "tp"), P(None, "tp", "sp"), P(None, "tp", "sp")),
        check_vma=False,
    )
```

```python
import functools
import math

import jax
import jax.numpy as jnp
from jax import lax
from jax.experimental import pallas as pl
from jax.experimental.pallas import tpu as pltpu
from jax.sharding import PartitionSpec as P

HS = 32
WS = 32
MESH = pl.DeviceIdType.MESH
F32 = jnp.float32
BF16 = jnp.bfloat16


def pad_frames(values):
    return jnp.pad(values, ((0, 0), (1, 1), (0, 0), (0, 0)))


def nt(a, b):
    return lax.dot_general(a, b, (((1,), (1,)), ((), ())), preferred_element_type=F32)


def nn(a, b):
    return lax.dot_general(a, b, (((1,), (0,)), ((), ())), preferred_element_type=F32)


def chunks_of(taps, size):
    return [(start, min(size, taps - start)) for start in range(0, taps, size)]


def order(chunks, first, images, tap_kb):
    hop, rate = 2.0, 45.0 / 1.0
    now, free = 0.0, {"core": 0.0, "x": 0.0, "z": 0.0, "back": 0.0}
    pending, out = {}, []

    def send(link, n, step):
        cost = chunks[n][1] * tap_kb / rate if link != "core" else chunks[n][1] * tap_kb / 100.0
        free[link] = max(free[link], now) + cost
        pending[step, n] = free[link] + hop

    for n in range(first):
        send("x", n, 2)
    grads, filler = list(range(first, len(chunks))), list(range(images))
    while pending or grads or filler:
        ready = sorted((at, key) for key, at in pending.items() if at <= now)
        if grads and (not ready or len(ready) < 2):
            n = grads.pop(0)
            out.append(("g", n))
            now += 0.6 * chunks[n][1]
            send("core", n, 1)
        elif ready or not filler:
            at, (step, n) = ready[0] if ready else min((at, key) for key, at in pending.items())
            now = max(now, at) + 0.12 * chunks[n][1]
            del pending[step, n]
            out.append((step, n))
            if step == 1:
                send("x", n, 2)
            elif step == 2:
                send("z", n, 3)
            elif step == 3:
                send("z", n, 4)
            elif step == 4:
                send("back", n, 5)
        else:
            n = filler.pop(0)
            out.append(("i", n))
            now += 0.7
    return out


def kernel(
    dims, lat, sav, og, tw, sw, ig, tg, sg,
    latv, savv, twv, swv, opad, hsend, hrecv, hwide, hs, savt, latt, acc,
    gsend, g1, g2s, g2r, gz, gzr, gf,
    lsem, osend, orecv, osem, hsendsem, hrecvsem, hlocsem,
    s1s, s1r, s2s, s2r, s3s, s3r,
):
    S, T, Z, F, Pl, Cl, Cs, scale, chunks, KT = dims
    U = S // 2
    HW = S * Pl
    C = T * Cl
    me_s, me_t, me_z = lax.axis_index("sp"), lax.axis_index("tp"), lax.axis_index("clip")
    me_u, me_c = me_s // 2, lax.rem(me_s, 2)

    loads = [
        pltpu.make_async_copy(src, dst, lsem.at[n])
        for n, (src, dst) in enumerate(((sav, savv), (tw, twv), (lat, latv), (sw, swv)))
    ]
    for copy in loads:
        copy.start()
    my_cols = pl.ds(pl.multiple_of(me_t * Cl, Cl), Cl)
    mine = [
        pltpu.make_async_copy(og.at[pl.ds(f * Pl, Pl)], opad.at[pl.ds((f + 1) * Pl, Pl), my_cols], osem.at[f])
        for f in range(F)
    ]
    for copy in mine:
        copy.start()

    barrier = pltpu.get_barrier_semaphore()
    count = 0
    for ds_ in range(S):
        for dt in range(T):
            if ds_ == 0 and dt == 0:
                continue
            count += 1
            pl.semaphore_signal(
                barrier, inc=1, device_id=(me_z, lax.rem(me_s + ds_, S), lax.rem(me_t + dt, T)),
                device_id_type=MESH,
            )
    for dz in range(1, Z):
        count += 1
        pl.semaphore_signal(
            barrier, inc=1, device_id=(lax.rem(me_z + dz, Z), me_s, me_t), device_id_type=MESH
        )
    pl.semaphore_wait(barrier, count)

    ocopies = []
    for d in range(F):
        f = lax.rem(me_s + d, F)
        ocopies.append([])
        for dt in range(1, T):
            copy = pltpu.make_async_remote_copy(
                src_ref=og.at[pl.ds(pl.multiple_of(f * Pl, Pl), Pl)],
                dst_ref=opad.at[pl.ds(pl.multiple_of((f + 1) * Pl, Pl), Pl), my_cols],
                send_sem=osend.at[d, dt - 1], recv_sem=orecv.at[d, dt - 1],
                device_id=(me_z, me_s, lax.rem(me_t + dt, T)), device_id_type=MESH,
            )
            copy.start()
            ocopies[-1].append(copy)

    opad[pl.ds(0, Pl), :] = jnp.zeros((Pl, C), BF16)
    opad[pl.ds((F + 1) * Pl, Pl), :] = jnp.zeros((Pl, C), BF16)
    hwide[pl.ds(0, 8), :] = jnp.zeros((8, C), F32)
    hwide[pl.ds(8 + HW, 8), :] = jnp.zeros((8, C), F32)
    for b in range(3):
        hs[b, pl.ds(0, WS), :] = jnp.zeros((WS, C), BF16)
        hs[b, pl.ds(WS + HW, WS), :] = jnp.zeros((WS, C), BF16)
    loads[0].wait()
    savt[...] = savv[...].T
    loads[2].wait()
    latt[...] = latv[...].T
    loads[1].wait()
    loads[3].wait()
    for copy in mine:
        copy.wait()
    arrived = set()

    hcopies = []
    for d in list(range(1, S)) + [0]:
        f = lax.rem(me_s + d, S)
        rows = pl.ds(pl.multiple_of(f * Pl, Pl), Pl)
        for need in range(d - 1, d + 2):
            if need % F not in arrived:
                arrived.add(need % F)
                for copy in ocopies[need % F]:
                    copy.wait()
        total = None
        for k in range(KT):
            moved = opad[pl.ds(pl.multiple_of((f + KT - 1 - k) * Pl, Pl), Pl), :]
            term = nt(moved, twv[k])
            total = term if total is None else total + term
        hsend[rows, :] = total.astype(BF16)
        dst = hrecv.at[pl.ds(pl.multiple_of(me_s * Pl, Pl), Pl), my_cols]
        for dt in range(T):
            if d == 0 and dt == 0:
                own = pltpu.make_async_copy(hsend.at[rows], dst, hlocsem)
                own.start()
                continue
            copy = pltpu.make_async_remote_copy(
                src_ref=hsend.at[rows], dst_ref=dst,
                send_sem=hsendsem.at[d, dt], recv_sem=hrecvsem.at[d, dt],
                device_id=(me_z, f, lax.rem(me_t + dt, T)), device_id_type=MESH,
            )
            copy.start()
            hcopies.append(copy)

    sent = {}

    def store_partial(tap, part):
        for s in range(S):
            gsend[s % 2, s // 2, tap] = part[:, s * Cs : (s + 1) * Cs].astype(BF16)

    def start1(n):
        at, size = chunks[n]
        copy = pltpu.make_async_remote_copy(
            src_ref=gsend.at[1 - me_c, :, pl.ds(at, size)], dst_ref=g1.at[:, pl.ds(at, size)],
            send_sem=s1s.at[n], recv_sem=s1r.at[n],
            device_id=(me_z, me_u * 2 + 1 - me_c, me_t), device_id_type=MESH,
        )
        copy.start()
        sent[1, n] = [copy]

    def step1(n):
        at, size = chunks[n]
        taps = pl.ds(at, size)
        for copy in sent[1, n]:
            copy.wait()
        g2s[:, taps] = (gsend[me_c, :, taps].astype(F32) + g1[:, taps].astype(F32)).astype(BF16)
        copies = []
        for d in range(1, U):
            other = lax.rem(me_u + d, U)
            copy = pltpu.make_async_remote_copy(
                src_ref=g2s.at[other, taps], dst_ref=g2r.at[d - 1, taps],
                send_sem=s2s.at[n, d - 1], recv_sem=s2r.at[n, d - 1],
                device_id=(me_z, other * 2 + me_c, me_t), device_id_type=MESH,
            )
            copy.start()
            copies.append(copy)
        sent[2, n] = copies

    def step2(n):
        at, size = chunks[n]
        taps = pl.ds(at, size)
        for copy in sent[2, n]:
            copy.wait()
        total = g2s[me_u, taps].astype(F32)
        for d in range(1, U):
            total = total + g2r[d - 1, taps].astype(F32)
        gz[taps] = total.astype(BF16)

        @pl.when(jnp.logical_and(is_end, jnp.logical_not(is_inner)))
        def _():
            to_inner(n).start()

    half = Z // 2
    low = me_z < half
    is_end = jnp.logical_or(me_z == 0, me_z == Z - 1)
    is_inner = jnp.logical_or(me_z == half - 1, me_z == half)
    z_in = jnp.where(low, me_z + 1, me_z - 1)
    z_out = jnp.clip(jnp.where(low, me_z - 1, me_z + 1), 0, Z - 1)
    Z_INNER, Z_OUTER = 0, 1

    def hop(n, src, slot, target):
        at, size = chunks[n]
        taps = pl.ds(at, size)
        return pltpu.make_async_remote_copy(
            src_ref=src.at[taps], dst_ref=gzr.at[slot, taps],
            send_sem=s3s.at[slot, n], recv_sem=s3r.at[slot, n],
            device_id=(target, me_s, me_t), device_id_type=MESH,
        )

    def to_inner(n):
        return hop(n, gz, Z_OUTER, z_in)

    def across(n):
        return hop(n, gz, Z_INNER, z_in)

    def to_outer(n):
        return hop(n, gf, Z_INNER, z_out)

    def step3(n):
        at, size = chunks[n]
        taps = pl.ds(at, size)

        @pl.when(jnp.logical_not(is_end))
        def _():
            to_inner(n).wait_recv()
            gz[taps] = (gz[taps].astype(F32) + gzr[Z_OUTER, taps].astype(F32)).astype(BF16)

            @pl.when(jnp.logical_not(is_inner))
            def _():
                to_inner(n).start()

        @pl.when(is_inner)
        def _():
            across(n).start()

    def output(n):
        at, size = chunks[n]
        value = gf[pl.ds(at, size)].astype(F32) * scale
        if at < KT:
            tg[pl.ds(at, size)] = value
        else:
            sg[pl.ds(at - KT, size)] = value

        @pl.when(jnp.logical_not(is_end))
        def _():
            to_outer(n).start()

    def step4(n):
        at, size = chunks[n]
        taps = pl.ds(at, size)

        @pl.when(is_inner)
        def _():
            across(n).wait_recv()
            gf[taps] = (gz[taps].astype(F32) + gzr[Z_INNER, taps].astype(F32)).astype(BF16)
            output(n)

    def step5(n):
        at, size = chunks[n]
        taps = pl.ds(at, size)

        @pl.when(jnp.logical_not(is_inner))
        def _():
            across(n).wait_recv()
            gf[taps] = gzr[Z_INNER, taps]
            output(n)

    def finish(n):
        @pl.when(is_inner)
        def _():
            across(n).wait_send()

        @pl.when(jnp.logical_not(is_inner))
        def _():
            to_inner(n).wait_send()

        @pl.when(jnp.logical_not(is_end))
        def _():
            to_outer(n).wait_send()

    first = len([0 for at, _ in chunks if at < KT])
    for n in range(first):
        at, size = chunks[n]

        @pl.loop(at, at + size)
        def _(k):
            moved = opad[pl.ds(pl.multiple_of((KT - 1 - k) * Pl, Pl), F * Pl), :]
            store_partial(k, nn(savt[...], moved))

        start1(n)
    own.wait()
    for copy in hcopies:
        copy.wait()

    for n in range(first):
        step1(n)

    tile = 4 * WS
    for r in range(0, HW, tile):
        hwide[pl.ds(8 + r, tile), :] = hrecv[pl.ds(r, tile), :].astype(F32)
        hs[1, pl.ds(WS + r, tile), :] = hrecv[pl.ds(r, tile), :]
    column = lax.rem(lax.broadcasted_iota(jnp.int32, (tile, C), 0), WS)
    for b in (-1, 1):
        keep = column != (0 if b == 1 else WS - 1)
        for r in range(0, HW, tile):
            value = hwide[pl.ds(8 + r - b, tile), :]
            hs[b + 1, pl.ds(WS + r, tile), :] = jnp.where(keep, value, 0.0).astype(BF16)

    def moved_at(tap):
        row, col = tap // 3, lax.rem(tap, 3)
        return hs[col, pl.ds(pl.multiple_of((2 - row) * WS, WS), HW), :]

    def gradient(n):
        at, size = chunks[n]

        @pl.loop(at - KT, at - KT + size)
        def _(tap):
            store_partial(tap + KT, nn(latt[...], moved_at(tap)))

        start1(n)

    taps_left = swv.shape[0]

    def image(tap):
        term = nt(moved_at(tap), swv[tap])
        if tap == 0:
            acc[...] = term
        elif tap < taps_left - 1:
            acc[...] += term
        else:
            ig[...] = (acc[...] + term).astype(BF16)

    steps = {1: step1, 2: step2, 3: step3, 4: step4, 5: step5}
    total = len(chunks)
    for kind, n in order(chunks, first, taps_left, Cl * Cs * 2e-3):
        if kind == "g":
            gradient(n)
        elif kind == "i":
            image(n)
        else:
            steps[kind](n)
    for n in range(total):
        finish(n)


def fused(sizes, chunk, latents, saved_input, out_grad, temporal_weight, spatial_weight):
    S, T, Z = sizes
    F, Pl, Cl = out_grad.shape[1:]
    KT, _, C = temporal_weight.shape
    taps = KT + spatial_weight.shape[0]
    HW = latents.shape[2]
    Cs = C // S
    U = S // 2
    scale = 1.0 / math.sqrt(Z * F * HS * WS)
    chunks = chunks_of(KT, chunk) + [(KT + at, n) for at, n in chunks_of(taps - KT, chunk)]
    N = len(chunks)
    dims = (S, T, Z, F, Pl, Cl, Cs, scale, chunks, KT)
    V = pltpu.VMEM
    D = pltpu.SemaphoreType.DMA
    hbm = pl.BlockSpec(memory_space=pl.ANY)
    vmem = pl.BlockSpec(memory_space=pltpu.VMEM)
    ig, tg, sg = pl.pallas_call(
        functools.partial(kernel, dims),
        out_shape=(
            jax.ShapeDtypeStruct((HW, Cl), BF16),
            jax.ShapeDtypeStruct((KT, Cl, Cs), F32),
            jax.ShapeDtypeStruct((taps - KT, Cl, Cs), F32),
        ),
        in_specs=[hbm] * 5,
        out_specs=(vmem,) * 3,
        scratch_shapes=[
            V((HW, Cl), BF16), V((F * Pl, Cl), BF16), V((KT, Cl, C), BF16), V((taps - KT, Cl, C), BF16),
            V(((F + 2) * Pl, C), BF16), V((F * Pl, Cl), BF16), V((HW, C), BF16),
            V((HW + 16, C), F32), V((3, HW + 2 * WS, C), BF16),
            V((Cl, F * Pl), BF16), V((Cl, HW), BF16), V((HW, Cl), F32),
            V((2, U, taps, Cl, Cs), BF16), V((U, taps, Cl, Cs), BF16), V((U, taps, Cl, Cs), BF16),
            V((U - 1, taps, Cl, Cs), BF16), V((taps, Cl, Cs), BF16), V((2, taps, Cl, Cs), BF16),
            V((taps, Cl, Cs), BF16),
            D((4,)), D((F, T - 1)), D((F, T - 1)), D((F,)), D((S, T)), D((S, T)), D(()),
            D((N,)), D((N,)), D((N, U - 1)), D((N, U - 1)),
            D((2, N)), D((2, N)),
        ],
        compiler_params=pltpu.CompilerParams(
            collective_id=0, has_side_effects=True, vmem_limit_bytes=60 * 2**20
        ),
    )(
        latents.reshape(HW, Cl), saved_input.reshape(F * Pl, Cl), out_grad.reshape(F * Pl, Cl),
        temporal_weight, spatial_weight,
    )
    return ig.reshape(latents.shape), tg, sg


def plain(latents, saved_input, out_grad, temporal_weight, spatial_weight):
    clips_all = latents.shape[0] * lax.axis_size("clip")
    frames_all = latents.shape[1] * lax.axis_size("sp")
    scale_factor = 1.0 / math.sqrt(clips_all * frames_all * HS * WS)
    frames_count = out_grad.shape[1]
    local_in = temporal_weight.shape[1]
    saved_padded = pad_frames(saved_input)
    block_in = lax.all_gather(out_grad, "tp", axis=3, tiled=True)
    padded = pad_frames(block_in)
    hidden_acc = jnp.zeros(out_grad.shape[:3] + (local_in,), F32)
    parts = []
    for tap_index in range(3):
        shifted = padded[:, 2 - tap_index : 2 - tap_index + frames_count]
        hidden_acc = hidden_acc + jnp.einsum(
            "bfpo,io->bfpi", shifted, temporal_weight[tap_index], preferred_element_type=F32
        )
        window = saved_padded[:, tap_index : tap_index + frames_count]
        parts.append(jnp.einsum("bfpi,bfpo->io", window, block_in, preferred_element_type=F32))
    temporal_local = jnp.stack(parts)
    hidden_grad = hidden_acc.astype(BF16)
    regrouped = lax.all_to_all(hidden_grad, "sp", split_axis=1, concat_axis=2, tiled=True)
    batch = latents.shape[0] * latents.shape[1]
    image_pad = jnp.pad(latents.reshape(batch, HS, WS, local_in), ((0, 0), (1, 1), (1, 1), (0, 0)))
    block_in = lax.all_gather(regrouped, "tp", axis=3, tiled=True)
    whole = block_in.reshape(batch, HS, WS, block_in.shape[3])
    grid = jnp.pad(whole, ((0, 0), (1, 1), (1, 1), (0, 0)))
    input_acc = jnp.zeros((batch, HS, WS, local_in), F32)
    parts = []
    for row in (-1, 0, 1):
        for col in (-1, 0, 1):
            tap_index = 3 * (row + 1) + (col + 1)
            moved = grid[:, 1 - row : 1 - row + HS, 1 - col : 1 - col + WS]
            input_acc = input_acc + jnp.einsum(
                "gabo,co->gabc", moved, spatial_weight[tap_index], preferred_element_type=F32
            )
            window = image_pad[:, 1 + row : 1 + row + HS, 1 + col : 1 + col + WS]
            parts.append(jnp.einsum("gabc,gabo->co", window, whole, preferred_element_type=F32))
    spatial_local = jnp.stack(parts)
    input_grad = input_acc.reshape(latents.shape).astype(BF16)
    temporal_grad, spatial_grad = lax.psum(
        tuple(
            lax.psum_scatter(value * scale_factor, "sp", scatter_dimension=2, tiled=True)
            for value in (temporal_local, spatial_local)
        ),
        "clip",
    )
    return input_grad, temporal_grad, spatial_grad


CHUNK = 1


def solution(mesh):
    sizes = (mesh.shape["sp"], mesh.shape["tp"], mesh.shape["clip"])

    def local(latents, saved_input, out_grad, temporal_weight, spatial_weight):
        S, T, Z = sizes
        cols = temporal_weight.shape[2] // S
        fits = (
            latents.shape[:2] == (1, 1) and S % 2 == 0 and S > 2 and T > 1 and Z % 2 == 0
            and cols % 128 == 0 and out_grad.shape[3] % 128 == 0
        )
        args = (latents, saved_input, out_grad, temporal_weight, spatial_weight)
        return fused(sizes, CHUNK, *args) if fits else plain(*args)

    return jax.shard_map(
        local,
        mesh=mesh,
        in_specs=(
            P("clip", "sp", None, "tp"),
            P("clip", None, "sp", "tp"),
            P("clip", None, "sp", "tp"),
            P(None, "tp", None),
            P(None, "tp", None),
        ),
        out_specs=(P("clip", "sp", None, "tp"), P(None, "tp", "sp"), P(None, "tp", "sp")),
        check_vma=False,
    )
```

```python
import functools
import math

import jax
import jax.numpy as jnp
from jax import lax
from jax.experimental import pallas as pl
from jax.experimental.pallas import tpu as pltpu
from jax.sharding import PartitionSpec as P

HS = 32
WS = 32
MESH = pl.DeviceIdType.MESH
F32 = jnp.float32
BF16 = jnp.bfloat16


def pad_frames(values):
    return jnp.pad(values, ((0, 0), (1, 1), (0, 0), (0, 0)))


def nt(a, b):
    return lax.dot_general(a, b, (((1,), (1,)), ((), ())), preferred_element_type=F32)


def nn(a, b):
    return lax.dot_general(a, b, (((1,), (0,)), ((), ())), preferred_element_type=F32)


def chunks_of(taps, size):
    return [(start, min(size, taps - start)) for start in range(0, taps, size)]


def order(chunks, first, images, tap_kb):
    hop, rate = 2.5, 40.0
    now, free = 0.0, {"core": 0.0, "x": 0.0, "z": 0.0, "back": 0.0}
    pending, out = {}, []

    def send(link, n, step):
        cost = chunks[n][1] * tap_kb / rate if link != "core" else chunks[n][1] * tap_kb / 100.0
        free[link] = max(free[link], now) + cost
        pending[step, n] = free[link] + hop

    for n in range(first):
        send("x", n, 2)
    grads, filler = list(range(first, len(chunks))), list(range(images))
    while pending or grads or filler:
        ready = sorted((at, key) for key, at in pending.items() if at <= now)
        if grads and (not ready or len(ready) < 2):
            n = grads.pop(0)
            out.append(("g", n))
            now += 0.8 * chunks[n][1]
            send("core", n, 1)
        elif ready or not filler:
            at, (step, n) = ready[0] if ready else min((at, key) for key, at in pending.items())
            now = max(now, at) + 0.12 * chunks[n][1]
            del pending[step, n]
            out.append((step, n))
            if step == 1:
                send("x", n, 2)
            elif step == 2:
                send("z", n, 3)
            elif step == 3:
                send("z", n, 4)
            elif step == 4:
                send("back", n, 5)
        else:
            n = filler.pop(0)
            out.append(("i", n))
            now += 0.7
    return out


def kernel(
    dims, lat, sav, og, tw, sw, ig, gf,
    latv, savv, twv, swv, opad, hsend, hrecv, hwide, hs, savt, latt, acc,
    gsend, g1, g2s, g2r, gz, gzf, gzr,
    lsem, osend, orecv, osem, hsendsem, hrecvsem, hlocsem,
    s1s, s1r, s2s, s2r, s3s, s3r,
):
    S, T, Z, F, Pl, Cl, Cs, scale, chunks, KT = dims
    U = S // 2
    HW = S * Pl
    C = T * Cl
    me_s, me_t, me_z = lax.axis_index("sp"), lax.axis_index("tp"), lax.axis_index("clip")
    me_u, me_c = me_s // 2, lax.rem(me_s, 2)

    loads = [
        pltpu.make_async_copy(src, dst, lsem.at[n])
        for n, (src, dst) in enumerate(((sav, savv), (tw, twv), (lat, latv), (sw, swv)))
    ]
    for copy in loads:
        copy.start()
    my_cols = pl.ds(pl.multiple_of(me_t * Cl, Cl), Cl)
    mine = [
        pltpu.make_async_copy(og.at[pl.ds(f * Pl, Pl)], opad.at[pl.ds((f + 1) * Pl, Pl), my_cols], osem.at[f])
        for f in range(F)
    ]
    for copy in mine:
        copy.start()

    barrier = pltpu.get_barrier_semaphore()
    count = 0
    for ds_ in range(S):
        for dt in range(T):
            if ds_ == 0 and dt == 0:
                continue
            count += 1
            pl.semaphore_signal(
                barrier, inc=1, device_id=(me_z, lax.rem(me_s + ds_, S), lax.rem(me_t + dt, T)),
                device_id_type=MESH,
            )
    for dz in range(1, Z):
        count += 1
        pl.semaphore_signal(
            barrier, inc=1, device_id=(lax.rem(me_z + dz, Z), me_s, me_t), device_id_type=MESH
        )
    pl.semaphore_wait(barrier, count)

    ocopies = []
    for d in range(F):
        f = lax.rem(me_s + d, F)
        ocopies.append([])
        for dt in range(1, T):
            copy = pltpu.make_async_remote_copy(
                src_ref=og.at[pl.ds(pl.multiple_of(f * Pl, Pl), Pl)],
                dst_ref=opad.at[pl.ds(pl.multiple_of((f + 1) * Pl, Pl), Pl), my_cols],
                send_sem=osend.at[d, dt - 1], recv_sem=orecv.at[d, dt - 1],
                device_id=(me_z, me_s, lax.rem(me_t + dt, T)), device_id_type=MESH,
            )
            copy.start()
            ocopies[-1].append(copy)

    opad[pl.ds(0, Pl), :] = jnp.zeros((Pl, C), BF16)
    opad[pl.ds((F + 1) * Pl, Pl), :] = jnp.zeros((Pl, C), BF16)
    hwide[pl.ds(0, 8), :] = jnp.zeros((8, C), F32)
    hwide[pl.ds(8 + HW, 8), :] = jnp.zeros((8, C), F32)
    for b in range(3):
        hs[b, pl.ds(0, WS), :] = jnp.zeros((WS, C), BF16)
        hs[b, pl.ds(WS + HW, WS), :] = jnp.zeros((WS, C), BF16)
    loads[0].wait()
    savt[...] = savv[...].T
    loads[2].wait()
    latt[...] = latv[...].T
    loads[1].wait()
    loads[3].wait()
    for copy in mine:
        copy.wait()
    arrived = set()

    hcopies = []
    for d in list(range(1, S)) + [0]:
        f = lax.rem(me_s + d, S)
        rows = pl.ds(pl.multiple_of(f * Pl, Pl), Pl)
        for need in range(d - 1, d + 2):
            if need % F not in arrived:
                arrived.add(need % F)
                for copy in ocopies[need % F]:
                    copy.wait()
        total = None
        for k in range(KT):
            moved = opad[pl.ds(pl.multiple_of((f + KT - 1 - k) * Pl, Pl), Pl), :]
            term = nt(moved, twv[k])
            total = term if total is None else total + term
        hsend[rows, :] = total.astype(BF16)
        dst = hrecv.at[pl.ds(pl.multiple_of(me_s * Pl, Pl), Pl), my_cols]
        for dt in range(T):
            if d == 0 and dt == 0:
                own = pltpu.make_async_copy(hsend.at[rows], dst, hlocsem)
                own.start()
                continue
            copy = pltpu.make_async_remote_copy(
                src_ref=hsend.at[rows], dst_ref=dst,
                send_sem=hsendsem.at[d, dt], recv_sem=hrecvsem.at[d, dt],
                device_id=(me_z, f, lax.rem(me_t + dt, T)), device_id_type=MESH,
            )
            copy.start()
            hcopies.append(copy)

    sent = {}

    def store_partial(tap, part):
        for s in range(S):
            gsend[s % 2, s // 2, tap] = part[:, s * Cs : (s + 1) * Cs].astype(BF16)

    def start1(n):
        at, size = chunks[n]
        copy = pltpu.make_async_remote_copy(
            src_ref=gsend.at[1 - me_c, :, pl.ds(at, size)], dst_ref=g1.at[:, pl.ds(at, size)],
            send_sem=s1s.at[n], recv_sem=s1r.at[n],
            device_id=(me_z, me_u * 2 + 1 - me_c, me_t), device_id_type=MESH,
        )
        copy.start()
        sent[1, n] = [copy]

    def step1(n):
        at, size = chunks[n]
        taps = pl.ds(at, size)
        for copy in sent[1, n]:
            copy.wait()
        g2s[:, taps] = (gsend[me_c, :, taps].astype(F32) + g1[:, taps].astype(F32)).astype(BF16)
        copies = []
        for d in range(1, U):
            other = lax.rem(me_u + d, U)
            copy = pltpu.make_async_remote_copy(
                src_ref=g2s.at[other, taps], dst_ref=g2r.at[d - 1, taps],
                send_sem=s2s.at[n, d - 1], recv_sem=s2r.at[n, d - 1],
                device_id=(me_z, other * 2 + me_c, me_t), device_id_type=MESH,
            )
            copy.start()
            copies.append(copy)
        sent[2, n] = copies

    def step2(n):
        at, size = chunks[n]
        taps = pl.ds(at, size)
        for copy in sent[2, n]:
            copy.wait()
        total = gsend[me_c, me_u, taps].astype(F32) + g1[me_u, taps].astype(F32)
        for d in range(1, U):
            total = total + g2r[d - 1, taps].astype(F32)
        gzf[taps] = total
        gz[taps] = total.astype(BF16)

        @pl.when(jnp.logical_and(is_end, jnp.logical_not(is_inner)))
        def _():
            to_inner(n).start()

    half = Z // 2
    low = me_z < half
    is_end = jnp.logical_or(me_z == 0, me_z == Z - 1)
    is_inner = jnp.logical_or(me_z == half - 1, me_z == half)
    z_in = jnp.where(low, me_z + 1, me_z - 1)
    z_out = jnp.clip(jnp.where(low, me_z - 1, me_z + 1), 0, Z - 1)
    Z_INNER, Z_OUTER = 0, 1

    def hop(n, src, slot, target):
        at, size = chunks[n]
        taps = pl.ds(at, size)
        return pltpu.make_async_remote_copy(
            src_ref=src.at[taps], dst_ref=gzr.at[slot, taps],
            send_sem=s3s.at[slot, n], recv_sem=s3r.at[slot, n],
            device_id=(target, me_s, me_t), device_id_type=MESH,
        )

    def to_inner(n):
        return hop(n, gz, Z_OUTER, z_in)

    def across(n):
        return hop(n, gz, Z_INNER, z_in)

    def to_outer(n):
        return hop(n, gf, Z_INNER, z_out)

    def step3(n):
        at, size = chunks[n]
        taps = pl.ds(at, size)

        @pl.when(jnp.logical_not(is_end))
        def _():
            to_inner(n).wait_recv()
            gz[taps] = (gzf[taps] + gzr[Z_OUTER, taps].astype(F32)).astype(BF16)

            @pl.when(jnp.logical_not(is_inner))
            def _():
                to_inner(n).start()

        @pl.when(is_inner)
        def _():
            across(n).start()

    def output(n):
        @pl.when(jnp.logical_not(is_end))
        def _():
            to_outer(n).start()

    def step4(n):
        at, size = chunks[n]
        taps = pl.ds(at, size)

        @pl.when(is_inner)
        def _():
            across(n).wait_recv()
            gf[taps] = (gz[taps].astype(F32) + gzr[Z_INNER, taps].astype(F32)).astype(BF16)
            output(n)

    def step5(n):
        at, size = chunks[n]
        taps = pl.ds(at, size)

        @pl.when(jnp.logical_not(is_inner))
        def _():
            across(n).wait_recv()
            gf[taps] = gzr[Z_INNER, taps]
            output(n)

    def finish(n):
        @pl.when(is_inner)
        def _():
            across(n).wait_send()

        @pl.when(jnp.logical_not(is_inner))
        def _():
            to_inner(n).wait_send()

        @pl.when(jnp.logical_not(is_end))
        def _():
            to_outer(n).wait_send()

    first = len([0 for at, _ in chunks if at < KT])
    for n in range(first):
        at, size = chunks[n]

        @pl.loop(at, at + size)
        def _(k):
            moved = opad[pl.ds(pl.multiple_of((KT - 1 - k) * Pl, Pl), F * Pl), :]
            store_partial(k, nn(savt[...], moved))

        start1(n)
    for n in range(first):
        step1(n)

    own.wait()
    for copy in hcopies:
        copy.wait()

    tile = 4 * WS
    for r in range(0, HW, tile):
        hwide[pl.ds(8 + r, tile), :] = hrecv[pl.ds(r, tile), :].astype(F32)
        hs[1, pl.ds(WS + r, tile), :] = hrecv[pl.ds(r, tile), :]
    column = lax.rem(lax.broadcasted_iota(jnp.int32, (tile, C), 0), WS)
    for b in (-1, 1):
        keep = column != (0 if b == 1 else WS - 1)
        for r in range(0, HW, tile):
            value = hwide[pl.ds(8 + r - b, tile), :]
            hs[b + 1, pl.ds(WS + r, tile), :] = jnp.where(keep, value, 0.0).astype(BF16)

    def moved_at(tap):
        row, col = tap // 3, lax.rem(tap, 3)
        return hs[col, pl.ds(pl.multiple_of((2 - row) * WS, WS), HW), :]

    def gradient(n):
        at, size = chunks[n]

        @pl.loop(at - KT, at - KT + size)
        def _(tap):
            store_partial(tap + KT, nn(latt[...], moved_at(tap)))

        start1(n)

    taps_left = swv.shape[0]

    def image(tap):
        term = nt(moved_at(tap), swv[tap])
        if tap == 0:
            acc[...] = term
        elif tap < taps_left - 1:
            acc[...] += term
        else:
            ig[...] = (acc[...] + term).astype(BF16)

    steps = {1: step1, 2: step2, 3: step3, 4: step4, 5: step5}
    total = len(chunks)
    for kind, n in order(chunks, first, taps_left, Cl * Cs * 2e-3):
        if kind == "g":
            gradient(n)
        elif kind == "i":
            image(n)
        else:
            steps[kind](n)
    for n in range(total):
        finish(n)


def fused(sizes, chunk, latents, saved_input, out_grad, temporal_weight, spatial_weight):
    S, T, Z = sizes
    F, Pl, Cl = out_grad.shape[1:]
    KT, _, C = temporal_weight.shape
    taps = KT + spatial_weight.shape[0]
    HW = latents.shape[2]
    Cs = C // S
    U = S // 2
    scale = 1.0 / math.sqrt(Z * F * HS * WS)
    chunks = chunks_of(KT, chunk) + [(KT + at, n) for at, n in chunks_of(taps - KT, chunk)]
    N = len(chunks)
    dims = (S, T, Z, F, Pl, Cl, Cs, scale, chunks, KT)
    V = pltpu.VMEM
    D = pltpu.SemaphoreType.DMA
    hbm = pl.BlockSpec(memory_space=pltpu.HBM)
    vmem = pl.BlockSpec(memory_space=pltpu.VMEM)
    ig, sums = pl.pallas_call(
        functools.partial(kernel, dims),
        out_shape=(
            jax.ShapeDtypeStruct((HW, Cl), BF16),
            jax.ShapeDtypeStruct((taps, Cl, Cs), BF16),
        ),
        in_specs=[hbm] * 5,
        out_specs=(vmem,) * 2,
        scratch_shapes=[
            V((HW, Cl), BF16), V((F * Pl, Cl), BF16), V((KT, Cl, C), BF16), V((taps - KT, Cl, C), BF16),
            V(((F + 2) * Pl, C), BF16), V((F * Pl, Cl), BF16), V((HW, C), BF16),
            V((HW + 16, C), F32), V((3, HW + 2 * WS, C), BF16),
            V((Cl, F * Pl), BF16), V((Cl, HW), BF16), V((HW, Cl), F32),
            V((2, U, taps, Cl, Cs), BF16), V((U, taps, Cl, Cs), BF16), V((U, taps, Cl, Cs), BF16),
            V((U - 1, taps, Cl, Cs), BF16), V((taps, Cl, Cs), BF16), V((taps, Cl, Cs), F32), V((2, taps, Cl, Cs), BF16),
            D((4,)), D((F, T - 1)), D((F, T - 1)), D((F,)), D((S, T)), D((S, T)), D(()),
            D((N,)), D((N,)), D((N, U - 1)), D((N, U - 1)),
            D((2, N)), D((2, N)),
        ],
        compiler_params=pltpu.CompilerParams(
            collective_id=0, has_side_effects=True, vmem_limit_bytes=63 * 2**20
        ),
    )(
        latents.reshape(HW, Cl), saved_input.reshape(F * Pl, Cl), out_grad.reshape(F * Pl, Cl),
        temporal_weight, spatial_weight,
    )

    def finish(ig_ref, sums_ref, ig_out, tg_out, sg_out):
        ig_out[...] = ig_ref[...]
        tg_out[...] = sums_ref[:KT].astype(F32) * scale
        sg_out[...] = sums_ref[KT:].astype(F32) * scale

    ig, tg, sg = pl.pallas_call(
        finish,
        out_shape=(
            jax.ShapeDtypeStruct((HW, Cl), BF16),
            jax.ShapeDtypeStruct((KT, Cl, Cs), F32),
            jax.ShapeDtypeStruct((taps - KT, Cl, Cs), F32),
        ),
        in_specs=[vmem] * 2,
        out_specs=(vmem,) * 3,
        compiler_params=pltpu.CompilerParams(vmem_limit_bytes=16 * 2**20),
    )(ig, sums)
    return ig.reshape(latents.shape), tg, sg


def plain(latents, saved_input, out_grad, temporal_weight, spatial_weight):
    clips_all = latents.shape[0] * lax.axis_size("clip")
    frames_all = latents.shape[1] * lax.axis_size("sp")
    scale_factor = 1.0 / math.sqrt(clips_all * frames_all * HS * WS)
    frames_count = out_grad.shape[1]
    local_in = temporal_weight.shape[1]
    saved_padded = pad_frames(saved_input)
    block_in = lax.all_gather(out_grad, "tp", axis=3, tiled=True)
    padded = pad_frames(block_in)
    hidden_acc = jnp.zeros(out_grad.shape[:3] + (local_in,), F32)
    parts = []
    for tap_index in range(3):
        shifted = padded[:, 2 - tap_index : 2 - tap_index + frames_count]
        hidden_acc = hidden_acc + jnp.einsum(
            "bfpo,io->bfpi", shifted, temporal_weight[tap_index], preferred_element_type=F32
        )
        window = saved_padded[:, tap_index : tap_index + frames_count]
        parts.append(jnp.einsum("bfpi,bfpo->io", window, block_in, preferred_element_type=F32))
    temporal_local = jnp.stack(parts)
    hidden_grad = hidden_acc.astype(BF16)
    regrouped = lax.all_to_all(hidden_grad, "sp", split_axis=1, concat_axis=2, tiled=True)
    batch = latents.shape[0] * latents.shape[1]
    image_pad = jnp.pad(latents.reshape(batch, HS, WS, local_in), ((0, 0), (1, 1), (1, 1), (0, 0)))
    block_in = lax.all_gather(regrouped, "tp", axis=3, tiled=True)
    whole = block_in.reshape(batch, HS, WS, block_in.shape[3])
    grid = jnp.pad(whole, ((0, 0), (1, 1), (1, 1), (0, 0)))
    input_acc = jnp.zeros((batch, HS, WS, local_in), F32)
    parts = []
    for row in (-1, 0, 1):
        for col in (-1, 0, 1):
            tap_index = 3 * (row + 1) + (col + 1)
            moved = grid[:, 1 - row : 1 - row + HS, 1 - col : 1 - col + WS]
            input_acc = input_acc + jnp.einsum(
                "gabo,co->gabc", moved, spatial_weight[tap_index], preferred_element_type=F32
            )
            window = image_pad[:, 1 + row : 1 + row + HS, 1 + col : 1 + col + WS]
            parts.append(jnp.einsum("gabc,gabo->co", window, whole, preferred_element_type=F32))
    spatial_local = jnp.stack(parts)
    input_grad = input_acc.reshape(latents.shape).astype(BF16)
    temporal_grad, spatial_grad = lax.psum(
        tuple(
            lax.psum_scatter(value * scale_factor, "sp", scatter_dimension=2, tiled=True)
            for value in (temporal_local, spatial_local)
        ),
        "clip",
    )
    return input_grad, temporal_grad, spatial_grad


CHUNK = 1


def solution(mesh):
    sizes = (mesh.shape["sp"], mesh.shape["tp"], mesh.shape["clip"])

    def local(latents, saved_input, out_grad, temporal_weight, spatial_weight):
        S, T, Z = sizes
        cols = temporal_weight.shape[2] // S
        fits = (
            latents.shape[:2] == (1, 1) and S % 2 == 0 and S > 2 and T > 1 and Z % 2 == 0
            and cols % 128 == 0 and out_grad.shape[3] % 128 == 0
        )
        args = (latents, saved_input, out_grad, temporal_weight, spatial_weight)
        return fused(sizes, CHUNK, *args) if fits else plain(*args)

    return jax.shard_map(
        local,
        mesh=mesh,
        in_specs=(
            P("clip", "sp", None, "tp"),
            P("clip", None, "sp", "tp"),
            P("clip", None, "sp", "tp"),
            P(None, "tp", None),
            P(None, "tp", None),
        ),
        out_specs=(P("clip", "sp", None, "tp"), P(None, "tp", "sp"), P(None, "tp", "sp")),
        check_vma=False,
    )
```

```python
import functools
import math

import jax
import jax.numpy as jnp
from jax import lax
from jax.experimental import pallas as pl
from jax.experimental.pallas import tpu as pltpu
from jax.sharding import PartitionSpec as P

HS = 32
WS = 32
MESH = pl.DeviceIdType.MESH
F32 = jnp.float32
BF16 = jnp.bfloat16


def pad_frames(values):
    return jnp.pad(values, ((0, 0), (1, 1), (0, 0), (0, 0)))


def nt(a, b):
    return lax.dot_general(a, b, (((1,), (1,)), ((), ())), preferred_element_type=F32)


def nn(a, b):
    return lax.dot_general(a, b, (((1,), (0,)), ((), ())), preferred_element_type=F32)


def chunks_of(taps, size):
    return [(start, min(size, taps - start)) for start in range(0, taps, size)]


def order(chunks, first, images, tap_kb):
    hop, rate = 2.5, 40.0
    now, free = 0.0, {"core": 0.0, "x": 0.0, "z": 0.0, "back": 0.0}
    pending, out = {}, []

    def send(link, n, step):
        cost = chunks[n][1] * tap_kb / rate if link != "core" else chunks[n][1] * tap_kb / 100.0
        free[link] = max(free[link], now) + cost
        pending[step, n] = free[link] + hop

    for n in range(first):
        send("z", n, 3)
    grads, filler = list(range(first, len(chunks))), list(range(images))
    while pending or grads or filler:
        ready = sorted((at, key) for key, at in pending.items() if at <= now)
        if grads and (not ready or len(ready) < 2):
            n = grads.pop(0)
            out.append(("g", n))
            now += 0.8 * chunks[n][1]
            send("core", n, 1)
        elif ready or not filler:
            at, (step, n) = ready[0] if ready else min((at, key) for key, at in pending.items())
            now = max(now, at) + 0.12 * chunks[n][1]
            del pending[step, n]
            out.append((step, n))
            if step == 1:
                send("x", n, 2)
            elif step == 2:
                send("z", n, 3)
            elif step == 3:
                send("z", n, 4)
            elif step == 4:
                send("back", n, 5)
        else:
            n = filler.pop(0)
            out.append(("i", n))
            now += 0.7
    return out


def kernel(
    dims, lat, sav, og, tw, sw, ig, gf,
    latv, savv, twv, swv, opad, hsend, hrecv, hwide, hs, savt, latt, acc,
    gsend, g1, g2s, g2r, gz, gzf, gzr,
    lsem, osend, orecv, osem, hsendsem, hrecvsem, hlocsem,
    s1s, s1r, s2s, s2r, s3s, s3r,
):
    S, T, Z, F, Pl, Cl, Cs, scale, chunks, KT = dims
    U = S // 2
    HW = S * Pl
    C = T * Cl
    me_s, me_t, me_z = lax.axis_index("sp"), lax.axis_index("tp"), lax.axis_index("clip")
    me_u, me_c = me_s // 2, lax.rem(me_s, 2)

    loads = [
        pltpu.make_async_copy(src, dst, lsem.at[n])
        for n, (src, dst) in enumerate(((sav, savv), (tw, twv), (lat, latv), (sw, swv)))
    ]
    for copy in loads:
        copy.start()
    my_cols = pl.ds(pl.multiple_of(me_t * Cl, Cl), Cl)
    mine = [
        pltpu.make_async_copy(og.at[pl.ds(f * Pl, Pl)], opad.at[pl.ds((f + 1) * Pl, Pl), my_cols], osem.at[f])
        for f in range(F)
    ]
    for copy in mine:
        copy.start()

    barrier = pltpu.get_barrier_semaphore()
    count = 0
    for ds_ in range(S):
        for dt in range(T):
            if ds_ == 0 and dt == 0:
                continue
            count += 1
            pl.semaphore_signal(
                barrier, inc=1, device_id=(me_z, lax.rem(me_s + ds_, S), lax.rem(me_t + dt, T)),
                device_id_type=MESH,
            )
    for dz in range(1, Z):
        count += 1
        pl.semaphore_signal(
            barrier, inc=1, device_id=(lax.rem(me_z + dz, Z), me_s, me_t), device_id_type=MESH
        )
    pl.semaphore_wait(barrier, count)

    ocopies = []
    for d in range(F):
        f = lax.rem(me_s + d, F)
        ocopies.append([])
        for dt in range(1, T):
            copy = pltpu.make_async_remote_copy(
                src_ref=og.at[pl.ds(pl.multiple_of(f * Pl, Pl), Pl)],
                dst_ref=opad.at[pl.ds(pl.multiple_of((f + 1) * Pl, Pl), Pl), my_cols],
                send_sem=osend.at[d, dt - 1], recv_sem=orecv.at[d, dt - 1],
                device_id=(me_z, me_s, lax.rem(me_t + dt, T)), device_id_type=MESH,
            )
            copy.start()
            ocopies[-1].append(copy)

    opad[pl.ds(0, Pl), :] = jnp.zeros((Pl, C), BF16)
    opad[pl.ds((F + 1) * Pl, Pl), :] = jnp.zeros((Pl, C), BF16)
    hwide[pl.ds(0, 8), :] = jnp.zeros((8, C), F32)
    hwide[pl.ds(8 + HW, 8), :] = jnp.zeros((8, C), F32)
    for b in range(3):
        hs[b, pl.ds(0, WS), :] = jnp.zeros((WS, C), BF16)
        hs[b, pl.ds(WS + HW, WS), :] = jnp.zeros((WS, C), BF16)
    loads[0].wait()
    savt[...] = savv[...].T
    loads[2].wait()
    latt[...] = latv[...].T
    loads[1].wait()
    loads[3].wait()
    for copy in mine:
        copy.wait()
    arrived = set()

    hcopies = []
    for d in list(range(1, S)) + [0]:
        f = lax.rem(me_s + d, S)
        rows = pl.ds(pl.multiple_of(f * Pl, Pl), Pl)
        for need in range(d - 1, d + 2):
            if need % F not in arrived:
                arrived.add(need % F)
                for copy in ocopies[need % F]:
                    copy.wait()
        total = None
        for k in range(KT):
            moved = opad[pl.ds(pl.multiple_of((f + KT - 1 - k) * Pl, Pl), Pl), :]
            term = nt(moved, twv[k])
            total = term if total is None else total + term
        hsend[rows, :] = total.astype(BF16)
        dst = hrecv.at[pl.ds(pl.multiple_of(me_s * Pl, Pl), Pl), my_cols]
        for dt in range(T):
            if d == 0 and dt == 0:
                own = pltpu.make_async_copy(hsend.at[rows], dst, hlocsem)
                own.start()
                continue
            copy = pltpu.make_async_remote_copy(
                src_ref=hsend.at[rows], dst_ref=dst,
                send_sem=hsendsem.at[d, dt], recv_sem=hrecvsem.at[d, dt],
                device_id=(me_z, f, lax.rem(me_t + dt, T)), device_id_type=MESH,
            )
            copy.start()
            hcopies.append(copy)

    sent = {}

    def store_partial(tap, part):
        for s in range(S):
            gsend[s % 2, s // 2, tap] = part[:, s * Cs : (s + 1) * Cs].astype(BF16)

    def start1(n):
        at, size = chunks[n]
        copy = pltpu.make_async_remote_copy(
            src_ref=gsend.at[1 - me_c, :, pl.ds(at, size)], dst_ref=g1.at[:, pl.ds(at, size)],
            send_sem=s1s.at[n], recv_sem=s1r.at[n],
            device_id=(me_z, me_u * 2 + 1 - me_c, me_t), device_id_type=MESH,
        )
        copy.start()
        sent[1, n] = [copy]

    def step1(n):
        at, size = chunks[n]
        taps = pl.ds(at, size)
        for copy in sent[1, n]:
            copy.wait()
        g2s[:, taps] = (gsend[me_c, :, taps].astype(F32) + g1[:, taps].astype(F32)).astype(BF16)
        copies = []
        for d in range(1, U):
            other = lax.rem(me_u + d, U)
            copy = pltpu.make_async_remote_copy(
                src_ref=g2s.at[other, taps], dst_ref=g2r.at[d - 1, taps],
                send_sem=s2s.at[n, d - 1], recv_sem=s2r.at[n, d - 1],
                device_id=(me_z, other * 2 + me_c, me_t), device_id_type=MESH,
            )
            copy.start()
            copies.append(copy)
        sent[2, n] = copies

    def step2(n):
        at, size = chunks[n]
        taps = pl.ds(at, size)
        for copy in sent[2, n]:
            copy.wait()
        total = gsend[me_c, me_u, taps].astype(F32) + g1[me_u, taps].astype(F32)
        for d in range(1, U):
            total = total + g2r[d - 1, taps].astype(F32)
        gzf[taps] = total
        gz[taps] = total.astype(BF16)

        @pl.when(jnp.logical_and(is_end, jnp.logical_not(is_inner)))
        def _():
            to_inner(n).start()

    half = Z // 2
    low = me_z < half
    is_end = jnp.logical_or(me_z == 0, me_z == Z - 1)
    is_inner = jnp.logical_or(me_z == half - 1, me_z == half)
    z_in = jnp.where(low, me_z + 1, me_z - 1)
    z_out = jnp.clip(jnp.where(low, me_z - 1, me_z + 1), 0, Z - 1)
    Z_INNER, Z_OUTER = 0, 1

    def hop(n, src, slot, target):
        at, size = chunks[n]
        taps = pl.ds(at, size)
        return pltpu.make_async_remote_copy(
            src_ref=src.at[taps], dst_ref=gzr.at[slot, taps],
            send_sem=s3s.at[slot, n], recv_sem=s3r.at[slot, n],
            device_id=(target, me_s, me_t), device_id_type=MESH,
        )

    def to_inner(n):
        return hop(n, gz, Z_OUTER, z_in)

    def across(n):
        return hop(n, gz, Z_INNER, z_in)

    def to_outer(n):
        return hop(n, gf, Z_INNER, z_out)

    def step3(n):
        at, size = chunks[n]
        taps = pl.ds(at, size)

        @pl.when(jnp.logical_not(is_end))
        def _():
            to_inner(n).wait_recv()
            gz[taps] = (gzf[taps] + gzr[Z_OUTER, taps].astype(F32)).astype(BF16)

            @pl.when(jnp.logical_not(is_inner))
            def _():
                to_inner(n).start()

        @pl.when(is_inner)
        def _():
            across(n).start()

    def output(n):
        @pl.when(jnp.logical_not(is_end))
        def _():
            to_outer(n).start()

    def step4(n):
        at, size = chunks[n]
        taps = pl.ds(at, size)

        @pl.when(is_inner)
        def _():
            across(n).wait_recv()
            gf[taps] = (gz[taps].astype(F32) + gzr[Z_INNER, taps].astype(F32)).astype(BF16)
            output(n)

    def step5(n):
        at, size = chunks[n]
        taps = pl.ds(at, size)

        @pl.when(jnp.logical_not(is_inner))
        def _():
            across(n).wait_recv()
            gf[taps] = gzr[Z_INNER, taps]
            output(n)

    def finish(n):
        @pl.when(is_inner)
        def _():
            across(n).wait_send()

        @pl.when(jnp.logical_not(is_inner))
        def _():
            to_inner(n).wait_send()

        @pl.when(jnp.logical_not(is_end))
        def _():
            to_outer(n).wait_send()

    first = len([0 for at, _ in chunks if at < KT])
    for n in range(first):
        at, size = chunks[n]

        @pl.loop(at, at + size)
        def _(k):
            moved = opad[pl.ds(pl.multiple_of((KT - 1 - k) * Pl, Pl), F * Pl), :]
            store_partial(k, nn(savt[...], moved))

        start1(n)
    for n in range(first):
        step1(n)
    for n in range(first):
        step2(n)

    own.wait()
    for copy in hcopies:
        copy.wait()

    tile = 4 * WS
    for r in range(0, HW, tile):
        hwide[pl.ds(8 + r, tile), :] = hrecv[pl.ds(r, tile), :].astype(F32)
        hs[1, pl.ds(WS + r, tile), :] = hrecv[pl.ds(r, tile), :]
    column = lax.rem(lax.broadcasted_iota(jnp.int32, (tile, C), 0), WS)
    for b in (-1, 1):
        keep = column != (0 if b == 1 else WS - 1)
        for r in range(0, HW, tile):
            value = hwide[pl.ds(8 + r - b, tile), :]
            hs[b + 1, pl.ds(WS + r, tile), :] = jnp.where(keep, value, 0.0).astype(BF16)

    def moved_at(tap):
        row, col = tap // 3, lax.rem(tap, 3)
        return hs[col, pl.ds(pl.multiple_of((2 - row) * WS, WS), HW), :]

    def gradient(n):
        at, size = chunks[n]

        @pl.loop(at - KT, at - KT + size)
        def _(tap):
            store_partial(tap + KT, nn(latt[...], moved_at(tap)))

        start1(n)

    taps_left = swv.shape[0]

    def image(tap):
        term = nt(moved_at(tap), swv[tap])
        if tap == 0:
            acc[...] = term
        elif tap < taps_left - 1:
            acc[...] += term
        else:
            ig[...] = (acc[...] + term).astype(BF16)

    steps = {1: step1, 2: step2, 3: step3, 4: step4, 5: step5}
    total = len(chunks)
    for kind, n in order(chunks, first, taps_left, Cl * Cs * 2e-3):
        if kind == "g":
            gradient(n)
        elif kind == "i":
            image(n)
        else:
            steps[kind](n)
    for n in range(total):
        finish(n)


def fused(sizes, chunk, latents, saved_input, out_grad, temporal_weight, spatial_weight):
    S, T, Z = sizes
    F, Pl, Cl = out_grad.shape[1:]
    KT, _, C = temporal_weight.shape
    taps = KT + spatial_weight.shape[0]
    HW = latents.shape[2]
    Cs = C // S
    U = S // 2
    scale = 1.0 / math.sqrt(Z * F * HS * WS)
    chunks = chunks_of(KT, chunk) + [(KT + at, n) for at, n in chunks_of(taps - KT, chunk)]
    N = len(chunks)
    dims = (S, T, Z, F, Pl, Cl, Cs, scale, chunks, KT)
    V = pltpu.VMEM
    D = pltpu.SemaphoreType.DMA
    hbm = pl.BlockSpec(memory_space=pltpu.HBM)
    vmem = pl.BlockSpec(memory_space=pltpu.VMEM)
    ig, sums = pl.pallas_call(
        functools.partial(kernel, dims),
        out_shape=(
            jax.ShapeDtypeStruct((HW, Cl), BF16),
            jax.ShapeDtypeStruct((taps, Cl, Cs), BF16),
        ),
        in_specs=[hbm] * 5,
        out_specs=(vmem,) * 2,
        scratch_shapes=[
            V((HW, Cl), BF16), V((F * Pl, Cl), BF16), V((KT, Cl, C), BF16), V((taps - KT, Cl, C), BF16),
            V(((F + 2) * Pl, C), BF16), V((F * Pl, Cl), BF16), V((HW, C), BF16),
            V((HW + 16, C), F32), V((3, HW + 2 * WS, C), BF16),
            V((Cl, F * Pl), BF16), V((Cl, HW), BF16), V((HW, Cl), F32),
            V((2, U, taps, Cl, Cs), BF16), V((U, taps, Cl, Cs), BF16), V((U, taps, Cl, Cs), BF16),
            V((U - 1, taps, Cl, Cs), BF16), V((taps, Cl, Cs), BF16), V((taps, Cl, Cs), F32), V((2, taps, Cl, Cs), BF16),
            D((4,)), D((F, T - 1)), D((F, T - 1)), D((F,)), D((S, T)), D((S, T)), D(()),
            D((N,)), D((N,)), D((N, U - 1)), D((N, U - 1)),
            D((2, N)), D((2, N)),
        ],
        compiler_params=pltpu.CompilerParams(
            collective_id=0, has_side_effects=True, vmem_limit_bytes=63 * 2**20
        ),
    )(
        latents.reshape(HW, Cl), saved_input.reshape(F * Pl, Cl), out_grad.reshape(F * Pl, Cl),
        temporal_weight, spatial_weight,
    )

    def finish(ig_ref, sums_ref, ig_out, tg_out, sg_out):
        ig_out[...] = ig_ref[...]
        tg_out[...] = sums_ref[:KT].astype(F32) * scale
        sg_out[...] = sums_ref[KT:].astype(F32) * scale

    ig, tg, sg = pl.pallas_call(
        finish,
        out_shape=(
            jax.ShapeDtypeStruct((HW, Cl), BF16),
            jax.ShapeDtypeStruct((KT, Cl, Cs), F32),
            jax.ShapeDtypeStruct((taps - KT, Cl, Cs), F32),
        ),
        in_specs=[vmem] * 2,
        out_specs=(vmem,) * 3,
        compiler_params=pltpu.CompilerParams(vmem_limit_bytes=16 * 2**20),
    )(ig, sums)
    return ig.reshape(latents.shape), tg, sg


def plain(latents, saved_input, out_grad, temporal_weight, spatial_weight):
    clips_all = latents.shape[0] * lax.axis_size("clip")
    frames_all = latents.shape[1] * lax.axis_size("sp")
    scale_factor = 1.0 / math.sqrt(clips_all * frames_all * HS * WS)
    frames_count = out_grad.shape[1]
    local_in = temporal_weight.shape[1]
    saved_padded = pad_frames(saved_input)
    block_in = lax.all_gather(out_grad, "tp", axis=3, tiled=True)
    padded = pad_frames(block_in)
    hidden_acc = jnp.zeros(out_grad.shape[:3] + (local_in,), F32)
    parts = []
    for tap_index in range(3):
        shifted = padded[:, 2 - tap_index : 2 - tap_index + frames_count]
        hidden_acc = hidden_acc + jnp.einsum(
            "bfpo,io->bfpi", shifted, temporal_weight[tap_index], preferred_element_type=F32
        )
        window = saved_padded[:, tap_index : tap_index + frames_count]
        parts.append(jnp.einsum("bfpi,bfpo->io", window, block_in, preferred_element_type=F32))
    temporal_local = jnp.stack(parts)
    hidden_grad = hidden_acc.astype(BF16)
    regrouped = lax.all_to_all(hidden_grad, "sp", split_axis=1, concat_axis=2, tiled=True)
    batch = latents.shape[0] * latents.shape[1]
    image_pad = jnp.pad(latents.reshape(batch, HS, WS, local_in), ((0, 0), (1, 1), (1, 1), (0, 0)))
    block_in = lax.all_gather(regrouped, "tp", axis=3, tiled=True)
    whole = block_in.reshape(batch, HS, WS, block_in.shape[3])
    grid = jnp.pad(whole, ((0, 0), (1, 1), (1, 1), (0, 0)))
    input_acc = jnp.zeros((batch, HS, WS, local_in), F32)
    parts = []
    for row in (-1, 0, 1):
        for col in (-1, 0, 1):
            tap_index = 3 * (row + 1) + (col + 1)
            moved = grid[:, 1 - row : 1 - row + HS, 1 - col : 1 - col + WS]
            input_acc = input_acc + jnp.einsum(
                "gabo,co->gabc", moved, spatial_weight[tap_index], preferred_element_type=F32
            )
            window = image_pad[:, 1 + row : 1 + row + HS, 1 + col : 1 + col + WS]
            parts.append(jnp.einsum("gabc,gabo->co", window, whole, preferred_element_type=F32))
    spatial_local = jnp.stack(parts)
    input_grad = input_acc.reshape(latents.shape).astype(BF16)
    temporal_grad, spatial_grad = lax.psum(
        tuple(
            lax.psum_scatter(value * scale_factor, "sp", scatter_dimension=2, tiled=True)
            for value in (temporal_local, spatial_local)
        ),
        "clip",
    )
    return input_grad, temporal_grad, spatial_grad


CHUNK = 1


def solution(mesh):
    sizes = (mesh.shape["sp"], mesh.shape["tp"], mesh.shape["clip"])

    def local(latents, saved_input, out_grad, temporal_weight, spatial_weight):
        S, T, Z = sizes
        cols = temporal_weight.shape[2] // S
        fits = (
            latents.shape[:2] == (1, 1) and S % 2 == 0 and S > 2 and T > 1 and Z % 2 == 0
            and cols % 128 == 0 and out_grad.shape[3] % 128 == 0
        )
        args = (latents, saved_input, out_grad, temporal_weight, spatial_weight)
        return fused(sizes, CHUNK, *args) if fits else plain(*args)

    return jax.shard_map(
        local,
        mesh=mesh,
        in_specs=(
            P("clip", "sp", None, "tp"),
            P("clip", None, "sp", "tp"),
            P("clip", None, "sp", "tp"),
            P(None, "tp", None),
            P(None, "tp", None),
        ),
        out_specs=(P("clip", "sp", None, "tp"), P(None, "tp", "sp"), P(None, "tp", "sp")),
        check_vma=False,
    )
```
